256 devices in a mesh: depth: 4 (over x_lo, core), tile: 64 (over y, z, x_hi).
Axes of the slice: x: 4 (x_hi: 2, x_lo: 2; x = x_hi * 2 + x_lo), y: 4, z: 8, core: 2. Of those that a mesh axis runs over, the one named last changes fastest.
Arguments:
- transmission: float32 [8, 2, 16384, 512], P('depth', None, 'tile'), may hold values from -5 to 5
- probe_field: float32 [2, 256, 256], replicated, may hold values from -5 to 5
- scan_positions: int32 [256, 2], P('tile'), may hold values from 0 to 16128, as said below
- amplitudes: float32 [256, 256, 256], P('tile'), may hold values from 0 to 3
Outputs:
- object_grad: float32 [8, 2, 16384, 512], P('depth', None, 'tile')
- probe_grad: float32 [2, 256, 256], P(None, 'depth')
The draws below stay inside these ranges and needn't reach their ends.
Inputs may be any that keep to these rules, and one draw needn't show every extreme that they name: `scan_positions`: column 0 holds a window's first row and column 1 its first column. The first row of window b lies in strip b // 4, that is between (b // 4) * 256 and (b // 4 + 1) * 256 - 1; windows of the last strip end inside the object, and a window's first column is at most 256.
All inputs are finite; a program needn't handle non-finite values.
Results may differ from the reference program's by a relative error of at most 0.0003.
Values sent between devices are 32-bit elements; how exact they have to be, the bound alone decides.
A program may use at most 128 MiB of HBM per device.

```python
import jax
import jax.numpy as jnp
from jax import lax

W = 256
TR = 256
NCOL = 512
WIN_TILE = 4
SLICES = 8
NROWS = 16384
NWIN = 256


def draw_scan_positions(key, part):
    row_key, col_key = jax.random.split(jax.random.fold_in(key, 17))
    window_ids = jnp.arange(NWIN, dtype=jnp.int32)
    strip_ids = window_ids // WIN_TILE
    last_strip = NWIN // WIN_TILE - 1
    row_span = jnp.where(strip_ids == last_strip, TR - W + 1, TR)
    row_offsets = jax.random.randint(row_key, (NWIN,), 0, 1 << 20, dtype=jnp.int32) % row_span
    col_offsets = jax.random.randint(col_key, (NWIN,), 0, NCOL - W + 1, dtype=jnp.int32)
    row_offsets = row_offsets.at[0].set(0).at[NWIN - 1].set(TR - W)
    col_offsets = col_offsets.at[0].set(0).at[NWIN - 1].set(NCOL - W)
    return jnp.stack([strip_ids * TR + row_offsets, col_offsets], axis=1).astype(jnp.int32)


def steps_of(rng, extent, cuts, smallest, largest):
    def one(axis_at, shards_of):
        steps = jax.random.uniform(jax.random.fold_in(jax.random.fold_in(rng, 6), axis_at), (shards_of,), jnp.float32, smallest / len(cuts), largest / len(cuts))
        return jnp.repeat(jnp.exp(steps), extent[axis_at] // shards_of).reshape((-1,) + (1,) * (len(extent) - axis_at - 1))

    loudness = one(*cuts[0])
    for cut in cuts[1:]:
        loudness = loudness * one(*cut)
    return loudness


def centred(stream_key, extent, scale, limit, cuts=(), kind=jnp.bfloat16):
    factor_of = steps_of(stream_key, extent, cuts, -0.22, 0.18) if cuts else 1.0
    result = jax.random.normal(stream_key, extent, jnp.float32) * scale * factor_of
    return jnp.minimum(jnp.maximum(result, -limit), limit).astype(kind)


def setup_inputs(seed: int = 0) -> dict:
    key_list = jax.random.split(jax.random.key(seed), 5)
    return {
        "transmission": centred(key_list[0], (SLICES, 2, NROWS, NCOL), 0.71, 5.0, ((0, 4), (2, 64)), jnp.float32),
        "probe_field": centred(key_list[1], (2, W, W), 0.71, 5.0, (), jnp.float32),
        "scan_positions": draw_scan_positions(jax.random.fold_in(key_list[4], 71), 0),
        "amplitudes": jnp.clip(3.0 * jax.random.uniform(key_list[3], (NWIN, W, W), jnp.float32) ** steps_of(key_list[3], (NWIN, W, W), ((0, 64),), -0.2, 0.2), 0.0, 3.0),
    }


def fresnel_kernel(length):
    indices = jnp.arange(length, dtype=jnp.int32)
    frequency = jnp.where(indices < length // 2, indices, indices - length).astype(jnp.float32)
    phase_angle = jnp.pi * frequency * frequency / (4.0 * length)
    factor_one = lax.complex(jnp.cos(phase_angle), -jnp.sin(phase_angle))
    return factor_one[:, None] * factor_one[None, :]

def reference(transmission, probe_field, scan_positions, amplitudes):
    kernel = fresnel_kernel(W)
    anchor = jnp.zeros((), jnp.int32)

    def one_window(carry_state, window_data):
        grad_total, probe_total = carry_state
        position, measured = window_data
        corner = (anchor, anchor, position[0].astype(jnp.int32), position[1].astype(jnp.int32))
        cropped = lax.dynamic_slice(transmission, corner, (SLICES, 2, W, W))
        trans_slices = lax.complex(cropped[:, 0], cropped[:, 1])
        wave_now = lax.complex(probe_field[0], probe_field[1])
        history = []
        for layer_index in range(SLICES):
            history.append(wave_now)
            wave_now = jnp.fft.ifft2(kernel * jnp.fft.fft2(trans_slices[layer_index] * wave_now))
        far_wave = jnp.fft.fft2(wave_now, norm='ortho')
        modulus = jnp.sqrt(jnp.real(far_wave) ** 2 + jnp.imag(far_wave) ** 2 + 1.0)
        grad_wave = jnp.fft.ifft2((1.0 - measured / modulus) * far_wave, norm='ortho')
        pieces = [None] * SLICES
        for layer_index in reversed(range(SLICES)):
            back_wave = jnp.fft.ifft2(jnp.conj(kernel) * jnp.fft.fft2(grad_wave))
            pieces[layer_index] = jnp.conj(history[layer_index]) * back_wave
            grad_wave = jnp.conj(trans_slices[layer_index]) * back_wave
        stacked = jnp.stack(pieces)
        update = jnp.stack([jnp.real(stacked), jnp.imag(stacked)], axis=1)
        current = lax.dynamic_slice(grad_total, corner, (SLICES, 2, W, W))
        grad_total = lax.dynamic_update_slice(grad_total, current + update, corner)
        probe_total = probe_total + jnp.stack([jnp.real(grad_wave), jnp.imag(grad_wave)])
        return ((grad_total, probe_total), None)
    start_state = (jnp.zeros_like(transmission), jnp.zeros_like(probe_field))
    (object_grad, probe_grad), unused = lax.scan(one_window, start_state, (scan_positions, amplitudes))
    return (object_grad, probe_grad)
```

```python
import jax
import jax.numpy as jnp
import ml_dtypes
import numpy as np
from jax import lax
from jax.experimental import pallas as pl
from jax.experimental.pallas import tpu as pltpu
from jax.sharding import PartitionSpec as P

MESH = pl.DeviceIdType.MESH
BF = jnp.bfloat16
F32 = jnp.float32
SIDE = 256
DEPTH = 4
WINDOWS = 4
NY, NZ, NX = 4, 8, 2
TILES = NY * NZ * NX
CH = 32
STEPS = SIDE // CH


def transform_tables():
    n = np.arange(SIDE)
    dft = np.exp(-2j * np.pi * ((n[:, None] * n[None, :]) % SIDE) / SIDE)
    m = np.where(n < SIDE // 2, n, n - SIDE).astype(np.float64)
    phase = np.exp(-1j * np.pi * m * m / (4 * SIDE))
    fresnel = (np.conj(dft) * phase[None, :]) @ dft / SIDE
    far = dft / np.sqrt(SIDE)
    pieces = []
    for table in (fresnel, far):
        for part in (table.real, table.imag):
            high = part.astype(np.float32).astype(ml_dtypes.bfloat16)
            low = (part - high.astype(np.float64)).astype(np.float32)
            pieces += [high, low.astype(ml_dtypes.bfloat16)]
    return np.stack(pieces).reshape(2, 4, SIDE, SIDE)


def halves(x):
    high = x.astype(BF)
    return high, (x - high.astype(F32)).astype(BF)


def thirds(x):
    high = x.astype(BF)
    rest = x - high.astype(F32)
    mid = rest.astype(BF)
    return high, mid, (rest - mid.astype(F32)).astype(BF)


def mega(
    trans, probe, pos, amp, tabs, obj, pgrad,
    own, rim, hist, gin, cbuf, acc, rimacc, rimg, left, right, dat, mid,
    ampv, probev, tabv, ptot, pscat, pin, zin, zsum, yin, ysum, xin, xsum, zout, pout,
    local_sem, rim_s, rim_r, fwd_s, fwd_r, bwd_s, bwd_r, rg_s, rg_r, obj_sem,
    ps_s, ps_r, z_s, z_r, y_s, y_r, x_s, x_r, yo_s, yo_r, zo_s, zo_r,
):
    d = lax.axis_index("depth")
    t = lax.axis_index("tile")
    xh = lax.rem(t, NX)
    z = lax.rem(lax.div(t, NX), NZ)
    y = lax.div(t, NX * NZ)
    above = lax.rem(t + TILES - 1, TILES)
    below = lax.rem(t + 1, TILES)

    def tile_of(yy, zz, xx):
        return (yy * NZ + zz) * NX + xx

    z_peers = [tile_of(y, lax.rem(z + i, NZ), xh) for i in range(1, NZ)]
    y_peers = [tile_of(lax.rem(y + i, NY), z, xh) for i in range(1, NY)]
    x_peer = tile_of(y, z, 1 - xh)

    barrier = pltpu.get_barrier_semaphore()
    peers = [{"tile": p} for p in [above, below] + z_peers + y_peers]
    peers += [{"depth": lax.rem(d + i, DEPTH)} for i in range(1, DEPTH)]
    for peer in peers:
        pl.semaphore_signal(barrier, inc=1, device_id=peer, device_id_type=MESH)
    pl.semaphore_wait(barrier, len(peers))

    def remote(src, dst, ss, rs, peer):
        return pltpu.make_async_remote_copy(src, dst, ss, rs, device_id=peer, device_id_type=MESH)

    def rim_copy(s):
        return remote(trans.at[s], rim.at[s], rim_s.at[s], rim_r.at[s], {"tile": above})

    def rim_grad_copy(s):
        return remote(rimacc.at[s], rimg.at[s], rg_s.at[s], rg_r.at[s], {"tile": below})

    def fwd_copy(w):
        return remote(hist.at[2, w], hist.at[0, w], fwd_s.at[w], fwd_r.at[w], {"depth": lax.rem(d + 1, DEPTH)})

    def bwd_copy(w):
        return remote(gin.at[w], gin.at[w], bwd_s.at[w], bwd_r.at[w], {"depth": lax.rem(d + DEPTH - 1, DEPTH)})

    for s in range(2):
        rim_copy(s).start()
    loads = [
        pltpu.make_async_copy(tabs, tabv, local_sem.at[0]),
        pltpu.make_async_copy(probe, probev, local_sem.at[1]),
        pltpu.make_async_copy(trans, own, local_sem.at[2]),
        pltpu.make_async_copy(amp, ampv, local_sem.at[3]),
    ]
    for load in loads:
        load.start()

    def clear(i, carry):
        rows = pl.ds(pl.multiple_of(i * CH, CH), CH)
        for s in range(2):
            for part in range(2):
                acc[s, part, rows, :] = jnp.zeros((CH, 2 * SIDE), F32)
                rimacc[s, part, rows, :] = jnp.zeros((CH, 2 * SIDE), F32)
        for part in range(2):
            ptot[part, rows, :] = jnp.zeros((CH, SIDE), F32)
        return carry

    lax.fori_loop(0, STEPS, clear, 0)
    loads[0].wait()
    for k in range(2):
        rh, rl, ih, il = tabv[k, 0], tabv[k, 1], tabv[k, 2], tabv[k, 3]
        for j, (a, b) in enumerate(((rh, ih), (rh, ih), (rl, il), (-ih, rh), (-ih, rh), (-il, rl))):
            span = slice(j * SIDE, (j + 1) * SIDE)
            left[k, :SIDE, span] = a
            left[k, SIDE:, span] = b
            right[k, span, :SIDE] = a
            right[k, span, SIDE:] = b
    loads[1].wait()
    loads[2].wait()
    loads[3].wait()

    def corner(w):
        return pos[w, 0] - t * SIDE, pos[w, 1]

    def one_hot(shift, flip):
        row = lax.broadcasted_iota(jnp.int32, (SIDE, SIDE), 0)
        col = lax.broadcasted_iota(jnp.int32, (SIDE, SIDE), 1)
        gap = (col - row) if flip else (row - col)
        return jnp.where(((gap - shift) & (SIDE - 1)) == 0, 1.0, 0.0).astype(BF)

    def rolled(x, rows, cols):
        a = sum(jnp.dot(rows, piece, preferred_element_type=F32) for piece in thirds(x))
        return sum(jnp.dot(piece, cols, preferred_element_type=F32) for piece in thirds(a))

    @pl.when(d == 0)
    def _():
        def place(w, carry):
            r, c = corner(w)
            rows, cols = one_hot(r, False), one_hot(c, True)
            for part in range(2):
                hist[0, w, part] = rolled(probev[part], rows, cols)
            return carry

        lax.fori_loop(0, WINDOWS, place, 0)

    def masks(i, w):
        r, c = corner(w)
        row = lax.broadcasted_iota(jnp.int32, (CH, SIDE), 0) + i * CH
        col = lax.broadcasted_iota(jnp.int32, (CH, SIDE), 1)
        return row >= r, col >= c

    def crop(s, rows, below_r, right_c):
        out = []
        for part in range(2):
            mine = jnp.where(right_c, own[s, part, rows, :SIDE], own[s, part, rows, SIDE:])
            theirs = jnp.where(right_c, rim[s, part, rows, :SIDE], rim[s, part, rows, SIDE:])
            out.append(jnp.where(below_r, mine, theirs))
        return out

    def put_data(i, re, im):
        re_h, re_l = halves(re)
        im_h, im_l = halves(im)
        for j, piece in enumerate((re_h, re_l, re_h, im_h, im_l, im_h)):
            dat[pl.ds(pl.multiple_of(j * SIDE + i * CH, CH), CH), :] = piece

    def sandwich(k):
        u = jnp.dot(left[k], dat[...], preferred_element_type=F32)
        re_h, re_l = halves(u[:SIDE])
        im_h, im_l = halves(u[SIDE:])
        for j, piece in enumerate((re_h, re_l, re_h, im_h, im_l, im_h)):
            mid[:, j * SIDE : (j + 1) * SIDE] = piece
        return jnp.dot(mid[...], right[k], preferred_element_type=F32)

    def forward(w):
        @pl.when(d > 0)
        def _():
            fwd_copy(w).wait_recv()

        def layer(s, carry):
            @pl.when(w == 0)
            def _():
                rim_copy(s).wait_recv()

            def chunk(i, carry2):
                rows = pl.ds(pl.multiple_of(i * CH, CH), CH)
                tr, ti = crop(s, rows, *masks(i, w))
                xr, xi = hist[s, w, 0, rows, :], hist[s, w, 1, rows, :]
                put_data(i, tr * xr - ti * xi, tr * xi + ti * xr)
                return carry2

            lax.fori_loop(0, STEPS, chunk, 0)
            v = sandwich(lax.div(d, 3) * s)
            hist[s + 1, w, 0] = v[:, :SIDE]
            hist[s + 1, w, 1] = v[:, SIDE:]
            return carry

        lax.fori_loop(0, 2, layer, 0)

        @pl.when(d < DEPTH - 1)
        def _():
            fwd_copy(w).start()

        @pl.when(d == DEPTH - 1)
        def _():
            def chunk(i, carry):
                rows = pl.ds(pl.multiple_of(i * CH, CH), CH)
                fr, fi = hist[2, w, 0, rows, :], hist[2, w, 1, rows, :]
                factor = 1.0 - ampv[w, rows, :] / jnp.sqrt(fr * fr + fi * fi + 1.0)
                gin[w, 0, rows, :] = factor * fr
                gin[w, 1, rows, :] = -(factor * fi)
                return carry

            lax.fori_loop(0, STEPS, chunk, 0)

    def backward(w):
        @pl.when(d < DEPTH - 1)
        def _():
            bwd_copy(w).wait_recv()

        def layer(j, carry):
            s = 1 - j

            def fill(i, carry2):
                rows = pl.ds(pl.multiple_of(i * CH, CH), CH)
                put_data(i, gin[w, 0, rows, :], gin[w, 1, rows, :])
                return carry2

            lax.fori_loop(0, STEPS, fill, 0)
            cbuf[...] = sandwich(lax.div(d, 3) * s)

            def chunk(i, carry2):
                rows = pl.ds(pl.multiple_of(i * CH, CH), CH)
                below_r, right_c = masks(i, w)
                tr, ti = crop(s, rows, below_r, right_c)
                br, bi = cbuf[rows, :SIDE], cbuf[rows, SIDE:]
                xr, xi = hist[s, w, 0, rows, :], hist[s, w, 1, rows, :]
                gin[w, 0, rows, :] = tr * br - ti * bi
                gin[w, 1, rows, :] = tr * bi + ti * br
                for part, piece in enumerate((xr * br - xi * bi, -(xr * bi + xi * br))):
                    mine = jnp.where(below_r, piece, 0.0)
                    theirs = jnp.where(below_r, 0.0, piece)
                    acc[s, part, rows, :SIDE] += jnp.where(right_c, mine, 0.0)
                    acc[s, part, rows, SIDE:] += jnp.where(right_c, 0.0, mine)
                    rimacc[s, part, rows, :SIDE] += jnp.where(right_c, theirs, 0.0)
                    rimacc[s, part, rows, SIDE:] += jnp.where(right_c, 0.0, theirs)
                return carry2

            lax.fori_loop(0, STEPS, chunk, 0)

            @pl.when(w == WINDOWS - 1)
            def _():
                rim_grad_copy(s).start()

            return carry

        lax.fori_loop(0, 2, layer, 0)

        @pl.when(d > 0)
        def _():
            bwd_copy(w).start()

        @pl.when(d == 0)
        def _():
            r, c = corner(w)
            rows, cols = one_hot(r, True), one_hot(c, False)
            ptot[0] += rolled(gin[w, 0], rows, cols)
            ptot[1] -= rolled(gin[w, 1], rows, cols)

    half = lax.div(d, 2)
    lag = (1 - half) * WINDOWS + half * (1 - lax.rem(d, 2))

    def step(k, carry):
        @pl.when(k < WINDOWS)
        def _():
            forward(k)

        b = k - lag

        @pl.when((b >= 0) & (b < WINDOWS))
        def _():
            backward(b)

        return carry

    lax.fori_loop(0, 2 * WINDOWS, step, 0)

    def scatter_copy(i):
        return remote(pscat.at[i], pin, ps_s.at[i - 1], ps_r.at[0], {"depth": i})

    tiles = [(q, q // 2, (q % 2) * 128) for q in range(4)]

    @pl.when(d == 0)
    def _():
        for owner in range(DEPTH):
            for p in range(NZ):
                top = owner * (SIDE // DEPTH) + p * 8
                for q, part, lane in tiles:
                    pscat[owner, p, q] = ptot[part, top : top + 8, lane : lane + 128]
        for owner in range(1, DEPTH):
            scatter_copy(owner).start()
        pin[...] = pscat[0]

    @pl.when(d > 0)
    def _():
        scatter_copy(1).wait_recv()

    for i in range(1, NZ):
        to = lax.rem(z + i, NZ)
        remote(pin.at[to], zin.at[i - 1], z_s.at[i - 1], z_r.at[i - 1], {"tile": z_peers[i - 1]}).start()
    total = pin[z]
    for i in range(1, NZ):
        remote(pin.at[0], zin.at[i - 1], z_s.at[i - 1], z_r.at[i - 1], {"tile": z_peers[i - 1]}).wait_recv()
        total = total + zin[i - 1]
    zsum[...] = total
    for i in range(1, NY):
        to = lax.rem(y + i, NY)
        remote(zsum.at[to], yin.at[i - 1], y_s.at[i - 1], y_r.at[i - 1], {"tile": y_peers[i - 1]}).start()
    total = zsum[y]
    for i in range(1, NY):
        remote(zsum.at[0], yin.at[i - 1], y_s.at[i - 1], y_r.at[i - 1], {"tile": y_peers[i - 1]}).wait_recv()
        total = total + yin[i - 1]
    ysum[...] = total
    exchange = remote(ysum, xin, x_s.at[0], x_r.at[0], {"tile": x_peer})
    exchange.start()
    exchange.wait_recv()
    total = total + xin[...]
    xsum[...] = total
    zout[y] = total
    y_back = [
        remote(xsum, zout.at[y], yo_s.at[i - 1], yo_r.at[i - 1], {"tile": y_peers[i - 1]}) for i in range(1, NY)
    ]
    for copy in y_back:
        copy.start()
    for copy in y_back:
        copy.wait_recv()
    pout[z] = zout[...]
    z_back = [
        remote(zout, pout.at[z], zo_s.at[i - 1], zo_r.at[i - 1], {"tile": z_peers[i - 1]}) for i in range(1, NZ)
    ]
    for copy in z_back:
        copy.start()
    for copy in z_back:
        copy.wait_recv()
    for p in range(NZ):
        for q, part, lane in tiles:
            pgrad[part, p * 8 : p * 8 + 8, lane : lane + 128] = pout[p, q]

    for s in (1, 0):
        rim_grad_copy(s).wait_recv()

        def finish(i, carry, s=s):
            rows = pl.ds(pl.multiple_of(i * CH, CH), CH)
            for part in range(2):
                acc[s, part, rows, :] += rimg[s, part, rows, :]
            return carry

        lax.fori_loop(0, STEPS, finish, 0)
        pltpu.make_async_copy(acc.at[s], obj.at[s], obj_sem.at[s]).start()
    for s in range(2):
        rim_copy(s).wait_send()
        rim_grad_copy(s).wait_send()

    @pl.when(d < DEPTH - 1)
    def _():
        for w in range(WINDOWS):
            fwd_copy(w).wait_send()

    @pl.when(d > 0)
    def _():
        for w in range(WINDOWS):
            bwd_copy(w).wait_send()

    @pl.when(d == 0)
    def _():
        for owner in range(1, DEPTH):
            scatter_copy(owner).wait_send()

    for i in range(1, NZ):
        remote(pin.at[0], zin.at[i - 1], z_s.at[i - 1], z_r.at[i - 1], {"tile": z_peers[i - 1]}).wait_send()
    for i in range(1, NY):
        remote(zsum.at[0], yin.at[i - 1], y_s.at[i - 1], y_r.at[i - 1], {"tile": y_peers[i - 1]}).wait_send()
    exchange.wait_send()
    for copy in y_back + z_back:
        copy.wait_send()
    for s in range(2):
        pltpu.make_async_copy(acc.at[s], obj.at[s], obj_sem.at[s]).wait()


def body(transmission, probe_field, scan_positions, amplitudes):
    tables = jnp.asarray(transform_tables())
    vm, dma = pltpu.VMEM, pltpu.SemaphoreType.DMA
    strip = (2, 2, SIDE, 2 * SIDE)
    anywhere = pl.BlockSpec(memory_space=pl.ANY)
    return pl.pallas_call(
        mega,
        out_shape=(
            jax.ShapeDtypeStruct(transmission.shape, F32),
            jax.ShapeDtypeStruct((2, SIDE // DEPTH, SIDE), F32),
        ),
        in_specs=[anywhere, anywhere, pl.BlockSpec(memory_space=pltpu.SMEM), anywhere, anywhere],
        out_specs=(anywhere, pl.BlockSpec(memory_space=pltpu.VMEM)),
        scratch_shapes=[
            vm(strip, F32),
            vm(strip, F32),
            vm((3, WINDOWS, 2, SIDE, SIDE), F32),
            vm((WINDOWS, 2, SIDE, SIDE), F32),
            vm((SIDE, 2 * SIDE), F32),
            vm(strip, F32),
            vm(strip, F32),
            vm(strip, F32),
            vm((2, 2 * SIDE, 6 * SIDE), BF),
            vm((2, 6 * SIDE, 2 * SIDE), BF),
            vm((6 * SIDE, SIDE), BF),
            vm((SIDE, 6 * SIDE), BF),
            vm((WINDOWS, SIDE, SIDE), F32),
            vm((2, SIDE, SIDE), F32),
            vm((2, 4, SIDE, SIDE), BF),
            vm((2, SIDE, SIDE), F32),
            vm((DEPTH, NZ, 4, 8, 128), F32),
            vm((NZ, 4, 8, 128), F32),
            vm((NZ - 1, 4, 8, 128), F32),
            vm((4, 8, 128), F32),
            vm((NY - 1, 8, 128), F32),
            vm((8, 128), F32),
            vm((8, 128), F32),
            vm((8, 128), F32),
            vm((4, 8, 128), F32),
            vm((NZ, 4, 8, 128), F32),
            dma((4,)),
            dma((2,)), dma((2,)),
            dma((4,)), dma((4,)),
            dma((4,)), dma((4,)),
            dma((2,)), dma((2,)),
            dma((2,)),
            dma((3,)), dma((1,)),
            dma((7,)), dma((7,)),
            dma((3,)), dma((3,)),
            dma((1,)), dma((1,)),
            dma((3,)), dma((3,)),
            dma((7,)), dma((7,)),
        ],
        compiler_params=pltpu.CompilerParams(
            collective_id=0, has_side_effects=True, vmem_limit_bytes=60 * 1024 * 1024
        ),
    )(transmission, probe_field, scan_positions, amplitudes, tables)


def solution(mesh):
    placed = (P("depth", None, "tile", None), P(), P("tile", None), P("tile", None, None))
    return jax.shard_map(
        body,
        mesh=mesh,
        in_specs=placed,
        out_specs=(P("depth", None, "tile", None), P(None, "depth", None)),
        check_vma=False,
    )
```

```python
import jax
import jax.numpy as jnp
import ml_dtypes
import numpy as np
from jax import lax
from jax.experimental import pallas as pl
from jax.experimental.pallas import tpu as pltpu
from jax.sharding import PartitionSpec as P

MESH = pl.DeviceIdType.MESH
BF = jnp.bfloat16
F32 = jnp.float32
SIDE = 256
DEPTH = 4
WINDOWS = 4
NY, NZ, NX = 4, 8, 2
TILES = NY * NZ * NX
CH = 32
STEPS = SIDE // CH


def transform_tables():
    n = np.arange(SIDE)
    dft = np.exp(-2j * np.pi * ((n[:, None] * n[None, :]) % SIDE) / SIDE)
    m = np.where(n < SIDE // 2, n, n - SIDE).astype(np.float64)
    phase = np.exp(-1j * np.pi * m * m / (4 * SIDE))
    fresnel = (np.conj(dft) * phase[None, :]) @ dft / SIDE
    far = dft / np.sqrt(SIDE)
    pieces = []
    for table in (fresnel, far):
        for part in (table.real, table.imag, table.real + table.imag):
            high = part.astype(np.float32).astype(ml_dtypes.bfloat16)
            low = (part - high.astype(np.float64)).astype(np.float32)
            pieces += [high, low.astype(ml_dtypes.bfloat16)]
    return np.stack(pieces).reshape(2, 6, SIDE, SIDE)


def halves(x):
    high = x.astype(BF)
    return high, (x - high.astype(F32)).astype(BF)


def thirds(x):
    high = x.astype(BF)
    rest = x - high.astype(F32)
    mid = rest.astype(BF)
    return high, mid, (rest - mid.astype(F32)).astype(BF)


def mega(
    trans, probe, pos, amp, tabs, obj, rimg, pgrad,
    own, rim, tmat, hist, gin, pieces, acc, rimacc, left, right, dat, mid,
    ampv, probev, tabv, ptot, pscat, pin, zin, zsum, yin, ysum, xin, xsum, zout, pout,
    local_sem, rim_s, rim_r, fwd_s, fwd_r, bwd_s, bwd_r, rg_s, rg_r, obj_sem,
    ps_s, ps_r, z_s, z_r, y_s, y_r, x_s, x_r, yo_s, yo_r, zo_s, zo_r, go,
):
    d = lax.axis_index("depth")
    t = lax.axis_index("tile")
    xh = lax.rem(t, NX)
    z = lax.rem(lax.div(t, NX), NZ)
    y = lax.div(t, NX * NZ)
    above = lax.rem(t + TILES - 1, TILES)
    below = lax.rem(t + 1, TILES)

    def tile_of(yy, zz, xx):
        return (yy * NZ + zz) * NX + xx

    z_peers = [tile_of(y, lax.rem(z + i, NZ), xh) for i in range(1, NZ)]
    y_peers = [tile_of(lax.rem(y + i, NY), z, xh) for i in range(1, NY)]
    x_peer = tile_of(y, z, 1 - xh)

    barrier = pltpu.get_barrier_semaphore()
    peers = [{"tile": p} for p in [above, below] + z_peers + y_peers]
    peers += [{"depth": lax.rem(d + i, DEPTH)} for i in range(1, DEPTH)]
    for peer in peers:
        pl.semaphore_signal(barrier, inc=1, device_id=peer, device_id_type=MESH)
    pl.semaphore_wait(barrier, len(peers))

    def remote(src, dst, ss, rs, peer):
        return pltpu.make_async_remote_copy(src, dst, ss, rs, device_id=peer, device_id_type=MESH)

    def rim_copy(s):
        return remote(trans.at[s], rim.at[s], rim_s.at[s], rim_r.at[s], {"tile": above})

    def rim_grad_copy(s):
        return remote(rimacc.at[s], rimg.at[s], rg_s.at[s], rg_r.at[s], {"tile": below})

    def fwd_copy(w):
        return remote(hist.at[2, w], hist.at[0, w], fwd_s.at[w], fwd_r.at[w], {"depth": lax.rem(d + 1, DEPTH)})

    def bwd_copy(w):
        return remote(gin.at[w], gin.at[w], bwd_s.at[w], bwd_r.at[w], {"depth": lax.rem(d + DEPTH - 1, DEPTH)})

    @pl.when(d != 1)
    def _():
        for s in range(2):
            rim_copy(s).start()

    loads = [
        pltpu.make_async_copy(tabs, tabv, local_sem.at[0]),
        pltpu.make_async_copy(probe, probev, local_sem.at[1]),
        pltpu.make_async_copy(trans, own, local_sem.at[2]),
        pltpu.make_async_copy(amp, ampv, local_sem.at[3]),
    ]
    for load in loads:
        load.start()

    def clear(i, carry):
        rows = pl.ds(pl.multiple_of(i * CH, CH), CH)
        for s in range(2):
            for part in range(2):
                acc[s, part, rows, :] = jnp.zeros((CH, 2 * SIDE), F32)
                rimacc[s, part, rows, :] = jnp.zeros((CH, 2 * SIDE), F32)
        for part in range(2):
            ptot[part, rows, :] = jnp.zeros((CH, SIDE), F32)
        return carry

    lax.fori_loop(0, STEPS, clear, 0)
    loads[0].wait()
    for k in range(2):
        for j in range(3):
            high, low = tabv[k, 2 * j], tabv[k, 2 * j + 1]
            for q, piece in enumerate((high, high, low)):
                span = slice((3 * j + q) * SIDE, (3 * j + q + 1) * SIDE)
                left[k, :, span] = piece
                right[k, span, :] = piece

    @pl.when(d == 0)
    def _():
        rim_copy(0).wait_send()
        pl.semaphore_signal(go, inc=1, device_id={"depth": 1}, device_id_type=MESH)

    @pl.when(d == 1)
    def _():
        pl.semaphore_wait(go, 1)
        for s in range(2):
            rim_copy(s).start()

    loads[1].wait()
    loads[2].wait()
    loads[3].wait()

    def corner(w):
        return pos[w, 0] - t * SIDE, pos[w, 1]

    def one_hot(shift, flip):
        row = lax.broadcasted_iota(jnp.int32, (SIDE, SIDE), 0)
        col = lax.broadcasted_iota(jnp.int32, (SIDE, SIDE), 1)
        gap = (col - row) if flip else (row - col)
        return jnp.where(((gap - shift) & (SIDE - 1)) == 0, 1.0, 0.0).astype(BF)

    def rolled(x, rows, cols):
        a = sum(jnp.dot(rows, piece, preferred_element_type=F32) for piece in thirds(x))
        return sum(jnp.dot(piece, cols, preferred_element_type=F32) for piece in thirds(a))

    @pl.when(d == 0)
    def _():
        def place(w, carry):
            r, c = corner(w)
            rows, cols = one_hot(r, False), one_hot(c, True)
            for part in range(2):
                hist[0, w, part] = rolled(probev[part], rows, cols)
            return carry

        lax.fori_loop(0, WINDOWS, place, 0)

    def masks(i, w):
        r, c = corner(w)
        row = lax.broadcasted_iota(jnp.int32, (CH, SIDE), 0) + i * CH
        col = lax.broadcasted_iota(jnp.int32, (CH, SIDE), 1)
        return row >= r, col >= c

    for s in range(2):
        rim_copy(s).wait_recv()

        def crop(w, carry, s=s):
            def chunk(i, carry2):
                rows = pl.ds(pl.multiple_of(i * CH, CH), CH)
                below_r, right_c = masks(i, w)
                for part in range(2):
                    mine = jnp.where(right_c, own[s, part, rows, :SIDE], own[s, part, rows, SIDE:])
                    theirs = jnp.where(right_c, rim[s, part, rows, :SIDE], rim[s, part, rows, SIDE:])
                    tmat[s, w, part, rows, :] = jnp.where(below_r, mine, theirs)
                return carry2

            return lax.fori_loop(0, STEPS, chunk, carry)

        lax.fori_loop(0, WINDOWS, crop, 0)

    def put(top, re, im):
        size = re.shape[0]
        for j, part in enumerate((re, im, re + im)):
            high, low = halves(part)
            for q, piece in enumerate((high, low, high)):
                start = (3 * j + q) * SIDE + top
                if not isinstance(top, int):
                    start = pl.multiple_of(start, CH)
                dat[pl.ds(start, size), :] = piece

    def dot(a, b):
        return jnp.dot(a, b, preferred_element_type=F32)

    K3 = 3 * SIDE
    HALF = SIDE // 2

    def sandwich(k, post):
        for m in range(2):
            rows = slice(m * HALF, (m + 1) * HALF)
            p1, p2, p3 = [
                dot(left[k, rows, j * K3 : (j + 1) * K3], dat[j * K3 : (j + 1) * K3, :]) for j in range(3)
            ]
            re = p1 - p2
            im = p3 - p1 - p2
            for j, part in enumerate((re, im, re + im)):
                high, low = halves(part)
                for q, piece in enumerate((high, low, high)):
                    mid[rows, (3 * j + q) * SIDE : (3 * j + q + 1) * SIDE] = piece
        for m in range(2):
            rows = slice(m * HALF, (m + 1) * HALF)
            p1, p2, p3 = [
                dot(mid[rows, j * K3 : (j + 1) * K3], right[k, j * K3 : (j + 1) * K3, :]) for j in range(3)
            ]
            re = p1 - p2
            im = p3 - p1 - p2
            for q in range(HALF // CH):
                post(m * HALF + q * CH, re[q * CH : (q + 1) * CH], im[q * CH : (q + 1) * CH])

    last = lax.div(d, 3)

    def forward(w):
        @pl.when(d > 0)
        def _():
            fwd_copy(w).wait_recv()

        def mix(i, carry):
            top = pl.multiple_of(i * CH, CH)
            rows = pl.ds(top, CH)
            tr, ti = tmat[0, w, 0, rows, :], tmat[0, w, 1, rows, :]
            xr, xi = hist[0, w, 0, rows, :], hist[0, w, 1, rows, :]
            put(top, tr * xr - ti * xi, tr * xi + ti * xr)
            return carry

        lax.fori_loop(0, STEPS, mix, 0)

        def next_mix(top, xr, xi):
            rows = slice(top, top + CH)
            hist[1, w, 0, rows, :] = xr
            hist[1, w, 1, rows, :] = xi
            tr, ti = tmat[1, w, 0, rows, :], tmat[1, w, 1, rows, :]
            put(top, tr * xr - ti * xi, tr * xi + ti * xr)

        sandwich(0, next_mix)

        def keep(top, xr, xi):
            rows = slice(top, top + CH)
            hist[2, w, 0, rows, :] = xr
            hist[2, w, 1, rows, :] = xi

        sandwich(last, keep)

        @pl.when(d < DEPTH - 1)
        def _():
            fwd_copy(w).start()

        @pl.when(d == DEPTH - 1)
        def _():
            def chunk(i, carry):
                rows = pl.ds(pl.multiple_of(i * CH, CH), CH)
                fr, fi = hist[2, w, 0, rows, :], hist[2, w, 1, rows, :]
                factor = 1.0 - ampv[w, rows, :] / jnp.sqrt(fr * fr + fi * fi + 1.0)
                gin[w, 0, rows, :] = factor * fr
                gin[w, 1, rows, :] = -(factor * fi)
                return carry

            lax.fori_loop(0, STEPS, chunk, 0)

    def backward(w):
        @pl.when(d < DEPTH - 1)
        def _():
            bwd_copy(w).wait_recv()

        def fill(i, carry):
            top = pl.multiple_of(i * CH, CH)
            rows = pl.ds(top, CH)
            put(top, gin[w, 0, rows, :], gin[w, 1, rows, :])
            return carry

        lax.fori_loop(0, STEPS, fill, 0)

        def unmix(s, top, br, bi):
            rows = slice(top, top + CH)
            xr, xi = hist[s, w, 0, rows, :], hist[s, w, 1, rows, :]
            pieces[s, 0, rows, :] = xr * br - xi * bi
            pieces[s, 1, rows, :] = -(xr * bi + xi * br)
            tr, ti = tmat[s, w, 0, rows, :], tmat[s, w, 1, rows, :]
            return tr * br - ti * bi, tr * bi + ti * br

        def upper(top, br, bi):
            put(top, *unmix(1, top, br, bi))

        def lower(top, br, bi):
            re, im = unmix(0, top, br, bi)
            rows = slice(top, top + CH)
            gin[w, 0, rows, :] = re
            gin[w, 1, rows, :] = im

        sandwich(last, upper)
        sandwich(0, lower)

        @pl.when(d > 0)
        def _():
            bwd_copy(w).start()

        @pl.when(d == 0)
        def _():
            r, c = corner(w)
            rows, cols = one_hot(r, True), one_hot(c, False)
            ptot[0] += rolled(gin[w, 0], rows, cols)
            ptot[1] -= rolled(gin[w, 1], rows, cols)

        @pl.when((d == 0) & (w == WINDOWS - 1))
        def _():
            scatter_probe()

        def gather(i, carry):
            rows = pl.ds(pl.multiple_of(i * CH, CH), CH)
            below_r, right_c = masks(i, w)
            for s in range(2):
                for part in range(2):
                    piece = pieces[s, part, rows, :]
                    mine = jnp.where(below_r, piece, 0.0)
                    theirs = jnp.where(below_r, 0.0, piece)
                    acc[s, part, rows, :SIDE] += jnp.where(right_c, mine, 0.0)
                    acc[s, part, rows, SIDE:] += jnp.where(right_c, 0.0, mine)
                    rimacc[s, part, rows, :SIDE] += jnp.where(right_c, theirs, 0.0)
                    rimacc[s, part, rows, SIDE:] += jnp.where(right_c, 0.0, theirs)
            return carry

        lax.fori_loop(0, STEPS, gather, 0)

    tiles = [(q, q // 2, (q % 2) * 128) for q in range(4)]

    def scatter_copy(i):
        return remote(pscat.at[i], pin, ps_s.at[i - 1], ps_r.at[0], {"depth": i})

    def scatter_probe():
        for owner in range(DEPTH):
            for p in range(NZ):
                top = owner * (SIDE // DEPTH) + p * 8
                for q, part, lane in tiles:
                    pscat[owner, p, q] = ptot[part, top : top + 8, lane : lane + 128]
        for owner in range(1, DEPTH):
            scatter_copy(owner).start()
        pin[...] = pscat[0]

    half = lax.div(d, 2)
    lag = (1 - half) * WINDOWS + half * (1 - lax.rem(d, 2))

    def step(k, carry):
        @pl.when(k < WINDOWS)
        def _():
            forward(k)

        b = k - lag

        @pl.when((b >= 0) & (b < WINDOWS))
        def _():
            backward(b)

        return carry

    lax.fori_loop(0, 2 * WINDOWS, step, 0)

    @pl.when(d == 2)
    def _():
        bwd_copy(WINDOWS - 1).wait_send()
        pl.semaphore_signal(go, inc=1, device_id={"depth": 3}, device_id_type=MESH)

    @pl.when(d == 3)
    def _():
        pl.semaphore_wait(go, 1)

    rim_grad_copy(1).start()
    for s in range(2):
        pltpu.make_async_copy(acc.at[s], obj.at[s], obj_sem.at[s]).start()

    @pl.when(d > 0)
    def _():
        scatter_copy(1).wait_recv()

    for i in range(1, NZ):
        to = lax.rem(z + i, NZ)
        remote(pin.at[to], zin.at[i - 1], z_s.at[i - 1], z_r.at[i - 1], {"tile": z_peers[i - 1]}).start()
    total = pin[z]
    for i in range(1, NZ):
        remote(pin.at[0], zin.at[i - 1], z_s.at[i - 1], z_r.at[i - 1], {"tile": z_peers[i - 1]}).wait_recv()
        total = total + zin[i - 1]
    zsum[...] = total
    for i in range(1, NY):
        to = lax.rem(y + i, NY)
        remote(zsum.at[to], yin.at[i - 1], y_s.at[i - 1], y_r.at[i - 1], {"tile": y_peers[i - 1]}).start()
    total = zsum[y]
    for i in range(1, NY):
        remote(zsum.at[0], yin.at[i - 1], y_s.at[i - 1], y_r.at[i - 1], {"tile": y_peers[i - 1]}).wait_recv()
        total = total + yin[i - 1]
    ysum[...] = total
    exchange = remote(ysum, xin, x_s.at[0], x_r.at[0], {"tile": x_peer})
    exchange.start()
    rim_grad_copy(0).start()
    exchange.wait_recv()
    total = total + xin[...]
    xsum[...] = total
    zout[y] = total
    y_back = [
        remote(xsum, zout.at[y], yo_s.at[i - 1], yo_r.at[i - 1], {"tile": y_peers[i - 1]}) for i in range(1, NY)
    ]
    for copy in y_back:
        copy.start()
    for copy in y_back:
        copy.wait_recv()
    pout[z] = zout[...]
    z_back = [
        remote(zout, pout.at[z], zo_s.at[i - 1], zo_r.at[i - 1], {"tile": z_peers[i - 1]}) for i in range(1, NZ)
    ]
    for copy in z_back:
        copy.start()
    for copy in z_back:
        copy.wait_recv()
    for p in range(NZ):
        for q, part, lane in tiles:
            pgrad[part, p * 8 : p * 8 + 8, lane : lane + 128] = pout[p, q]

    for s in (1, 0):
        rim_grad_copy(s).wait_recv()

    @pl.when(d > 0)
    def _():
        rim_copy(0).wait_send()

    rim_copy(1).wait_send()
    for s in range(2):
        rim_grad_copy(s).wait_send()

    @pl.when(d < DEPTH - 1)
    def _():
        for w in range(WINDOWS):
            fwd_copy(w).wait_send()

    @pl.when(d > 0)
    def _():
        for w in range(WINDOWS - 1):
            bwd_copy(w).wait_send()

    @pl.when((d == 1) | (d == 3))
    def _():
        bwd_copy(WINDOWS - 1).wait_send()

    @pl.when(d == 0)
    def _():
        for owner in range(1, DEPTH):
            scatter_copy(owner).wait_send()

    for i in range(1, NZ):
        remote(pin.at[0], zin.at[i - 1], z_s.at[i - 1], z_r.at[i - 1], {"tile": z_peers[i - 1]}).wait_send()
    for i in range(1, NY):
        remote(zsum.at[0], yin.at[i - 1], y_s.at[i - 1], y_r.at[i - 1], {"tile": y_peers[i - 1]}).wait_send()
    exchange.wait_send()
    for copy in y_back + z_back:
        copy.wait_send()
    for s in range(2):
        pltpu.make_async_copy(acc.at[s], obj.at[s], obj_sem.at[s]).wait()


def body(transmission, probe_field, scan_positions, amplitudes):
    tables = jnp.asarray(transform_tables())
    vm, dma = pltpu.VMEM, pltpu.SemaphoreType.DMA
    strip = (2, 2, SIDE, 2 * SIDE)
    anywhere = pl.BlockSpec(memory_space=pl.ANY)
    own_terms, rim_terms, probe_grad = pl.pallas_call(
        mega,
        out_shape=(
            jax.ShapeDtypeStruct(transmission.shape, F32),
            jax.ShapeDtypeStruct(transmission.shape, F32),
            jax.ShapeDtypeStruct((2, SIDE // DEPTH, SIDE), F32),
        ),
        in_specs=[anywhere, anywhere, pl.BlockSpec(memory_space=pltpu.SMEM), anywhere, anywhere],
        out_specs=(anywhere, anywhere, pl.BlockSpec(memory_space=pltpu.VMEM)),
        scratch_shapes=[
            vm(strip, F32),
            vm(strip, F32),
            vm((2, WINDOWS, 2, SIDE, SIDE), F32),
            vm((3, WINDOWS, 2, SIDE, SIDE), F32),
            vm((WINDOWS, 2, SIDE, SIDE), F32),
            vm((2, 2, SIDE, SIDE), F32),
            vm(strip, F32),
            vm(strip, F32),
            vm((2, SIDE, 9 * SIDE), BF),
            vm((2, 9 * SIDE, SIDE), BF),
            vm((9 * SIDE, SIDE), BF),
            vm((SIDE, 9 * SIDE), BF),
            vm((WINDOWS, SIDE, SIDE), F32),
            vm((2, SIDE, SIDE), F32),
            vm((2, 6, SIDE, SIDE), BF),
            vm((2, SIDE, SIDE), F32),
            vm((DEPTH, NZ, 4, 8, 128), F32),
            vm((NZ, 4, 8, 128), F32),
            vm((NZ - 1, 4, 8, 128), F32),
            vm((4, 8, 128), F32),
            vm((NY - 1, 8, 128), F32),
            vm((8, 128), F32),
            vm((8, 128), F32),
            vm((8, 128), F32),
            vm((4, 8, 128), F32),
            vm((NZ, 4, 8, 128), F32),
            dma((4,)),
            dma((2,)), dma((2,)),
            dma((4,)), dma((4,)),
            dma((4,)), dma((4,)),
            dma((2,)), dma((2,)),
            dma((2,)),
            dma((3,)), dma((1,)),
            dma((7,)), dma((7,)),
            dma((3,)), dma((3,)),
            dma((1,)), dma((1,)),
            dma((3,)), dma((3,)),
            dma((7,)), dma((7,)),
            pltpu.SemaphoreType.REGULAR,
        ],
        compiler_params=pltpu.CompilerParams(
            collective_id=0, has_side_effects=True, vmem_limit_bytes=60 * 1024 * 1024
        ),
    )(transmission, probe_field, scan_positions, amplitudes, tables)
    return own_terms + rim_terms, probe_grad


def solution(mesh):
    placed = (P("depth", None, "tile", None), P(), P("tile", None), P("tile", None, None))
    return jax.shard_map(
        body,
        mesh=mesh,
        in_specs=placed,
        out_specs=(P("depth", None, "tile", None), P(None, "depth", None)),
        check_vma=False,
    )
```

```python
import jax
import jax.numpy as jnp
import ml_dtypes
import numpy as np
from jax import lax
from jax.experimental import pallas as pl
from jax.experimental.pallas import tpu as pltpu
from jax.sharding import PartitionSpec as P

MESH = pl.DeviceIdType.MESH
BF = jnp.bfloat16
F32 = jnp.float32
SIDE = 256
DEPTH = 4
WINDOWS = 4
NY, NZ, NX = 4, 8, 2
TILES = NY * NZ * NX
CH = 32
STEPS = SIDE // CH


def transform_tables():
    n = np.arange(SIDE)
    dft = np.exp(-2j * np.pi * ((n[:, None] * n[None, :]) % SIDE) / SIDE)
    m = np.where(n < SIDE // 2, n, n - SIDE).astype(np.float64)
    phase = np.exp(-1j * np.pi * m * m / (4 * SIDE))
    fresnel = (np.conj(dft) * phase[None, :]) @ dft / SIDE
    far = dft / np.sqrt(SIDE)
    pieces = []
    for table in (fresnel, far):
        for part in (table.real, table.imag, table.real + table.imag):
            high = part.astype(np.float32).astype(ml_dtypes.bfloat16)
            low = (part - high.astype(np.float64)).astype(np.float32)
            pieces += [high, low.astype(ml_dtypes.bfloat16)]
    return np.stack(pieces).reshape(2, 6, SIDE, SIDE)


def halves(x):
    high = x.astype(BF)
    return high, (x - high.astype(F32)).astype(BF)


def thirds(x):
    high = x.astype(BF)
    rest = x - high.astype(F32)
    mid = rest.astype(BF)
    return high, mid, (rest - mid.astype(F32)).astype(BF)


def mega(
    trans, probe, pos, amp, tabs, obj, rimg, pgrad,
    own, rim, tmat, hist, gin, pieces, acc, rimacc, left, right, dat, mid,
    ampv, probev, tabv, ptot, pscat, pin, zin, zsum, yin, ysum, xin, xsum, zout, pout,
    local_sem, rim_s, rim_r, fwd_s, fwd_r, bwd_s, bwd_r, rg_s, rg_r, obj_sem,
    ps_s, ps_r, z_s, z_r, y_s, y_r, x_s, x_r, yo_s, yo_r, zo_s, zo_r, go,
):
    d = lax.axis_index("depth")
    t = lax.axis_index("tile")
    xh = lax.rem(t, NX)
    z = lax.rem(lax.div(t, NX), NZ)
    y = lax.div(t, NX * NZ)
    above = lax.rem(t + TILES - 1, TILES)
    below = lax.rem(t + 1, TILES)

    def tile_of(yy, zz, xx):
        return (yy * NZ + zz) * NX + xx

    z_peers = [tile_of(y, lax.rem(z + i, NZ), xh) for i in range(1, NZ)]
    y_peers = [tile_of(lax.rem(y + i, NY), z, xh) for i in range(1, NY)]
    x_peer = tile_of(y, z, 1 - xh)

    barrier = pltpu.get_barrier_semaphore()
    above2 = lax.rem(t + TILES - 2, TILES)
    below2 = lax.rem(t + 2, TILES)
    peers = [{"tile": p} for p in [above, below, above2, below2] + z_peers + y_peers]
    peers += [{"depth": lax.rem(d + i, DEPTH)} for i in range(1, DEPTH)]
    for peer in peers:
        pl.semaphore_signal(barrier, inc=1, device_id=peer, device_id_type=MESH)
    pl.semaphore_wait(barrier, len(peers))

    def remote(src, dst, ss, rs, peer):
        return pltpu.make_async_remote_copy(src, dst, ss, rs, device_id=peer, device_id_type=MESH)

    def rim_copy(s):
        return remote(trans.at[s], rim.at[s], rim_s.at[s], rim_r.at[s], {"tile": above})

    def rim_grad_copy(s):
        return remote(rimacc.at[s], rimg.at[s], rg_s.at[s], rg_r.at[s], {"tile": below})

    def fwd_copy(w):
        return remote(hist.at[2, w], hist.at[0, w], fwd_s.at[w], fwd_r.at[w], {"depth": lax.rem(d + 1, DEPTH)})

    def bwd_copy(w):
        return remote(gin.at[w], gin.at[w], bwd_s.at[w], bwd_r.at[w], {"depth": lax.rem(d + DEPTH - 1, DEPTH)})

    @pl.when(d != 1)
    def _():
        for s in range(2):
            rim_copy(s).start()

    loads = [
        pltpu.make_async_copy(tabs, tabv, local_sem.at[0]),
        pltpu.make_async_copy(probe, probev, local_sem.at[1]),
        pltpu.make_async_copy(trans, own, local_sem.at[2]),
        pltpu.make_async_copy(amp, ampv, local_sem.at[3]),
    ]
    for load in loads:
        load.start()

    def clear(i, carry):
        rows = pl.ds(pl.multiple_of(i * CH, CH), CH)
        for s in range(2):
            for part in range(2):
                acc[s, part, rows, :] = jnp.zeros((CH, 2 * SIDE), F32)
                rimacc[s, part, rows, :] = jnp.zeros((CH, 2 * SIDE), F32)
        for part in range(2):
            ptot[part, rows, :] = jnp.zeros((CH, SIDE), F32)
        return carry

    lax.fori_loop(0, STEPS, clear, 0)
    loads[0].wait()
    for k in range(2):
        for j in range(3):
            high, low = tabv[k, 2 * j], tabv[k, 2 * j + 1]
            for q, piece in enumerate((high, high, low)):
                span = slice((3 * j + q) * SIDE, (3 * j + q + 1) * SIDE)
                left[k, :, span] = piece
                right[k, span, :] = piece

    @pl.when(d == 0)
    def _():
        rim_copy(0).wait_send()
        pl.semaphore_signal(go, inc=1, device_id={"depth": 1}, device_id_type=MESH)

    @pl.when(d == 1)
    def _():
        pl.semaphore_wait(go, 1)
        for s in range(2):
            rim_copy(s).start()

    loads[1].wait()
    loads[2].wait()
    loads[3].wait()

    def corner(w):
        return pos[w, 0] - t * SIDE, pos[w, 1]

    def one_hot(shift, flip):
        row = lax.broadcasted_iota(jnp.int32, (SIDE, SIDE), 0)
        col = lax.broadcasted_iota(jnp.int32, (SIDE, SIDE), 1)
        gap = (col - row) if flip else (row - col)
        return jnp.where(((gap - shift) & (SIDE - 1)) == 0, 1.0, 0.0).astype(BF)

    def rolled(x, rows, cols):
        a = sum(jnp.dot(rows, piece, preferred_element_type=F32) for piece in thirds(x))
        return sum(jnp.dot(piece, cols, preferred_element_type=F32) for piece in thirds(a))

    @pl.when(d == 0)
    def _():
        def place(w, carry):
            r, c = corner(w)
            rows, cols = one_hot(r, False), one_hot(c, True)
            for part in range(2):
                hist[0, w, part] = rolled(probev[part], rows, cols)
            return carry

        lax.fori_loop(0, WINDOWS, place, 0)

    def masks(i, w):
        r, c = corner(w)
        row = lax.broadcasted_iota(jnp.int32, (CH, SIDE), 0) + i * CH
        col = lax.broadcasted_iota(jnp.int32, (CH, SIDE), 1)
        return row >= r, col >= c

    for s in range(2):
        rim_copy(s).wait_recv()

        def crop(w, carry, s=s):
            def chunk(i, carry2):
                rows = pl.ds(pl.multiple_of(i * CH, CH), CH)
                below_r, right_c = masks(i, w)
                for part in range(2):
                    mine = jnp.where(right_c, own[s, part, rows, :SIDE], own[s, part, rows, SIDE:])
                    theirs = jnp.where(right_c, rim[s, part, rows, :SIDE], rim[s, part, rows, SIDE:])
                    tmat[s, w, part, rows, :] = jnp.where(below_r, mine, theirs)
                return carry2

            return lax.fori_loop(0, STEPS, chunk, carry)

        lax.fori_loop(0, WINDOWS, crop, 0)

    def put(top, re, im):
        size = re.shape[0]
        for j, part in enumerate((re, im, re + im)):
            high, low = halves(part)
            for q, piece in enumerate((high, low, high)):
                start = (3 * j + q) * SIDE + top
                if not isinstance(top, int):
                    start = pl.multiple_of(start, CH)
                dat[pl.ds(start, size), :] = piece

    def dot(a, b):
        return jnp.dot(a, b, preferred_element_type=F32)

    K3 = 3 * SIDE
    HALF = SIDE // 2

    def sandwich(k, post):
        for m in range(2):
            rows = slice(m * HALF, (m + 1) * HALF)
            p1, p2, p3 = [
                dot(left[k, rows, j * K3 : (j + 1) * K3], dat[j * K3 : (j + 1) * K3, :]) for j in range(3)
            ]
            re = p1 - p2
            im = p3 - p1 - p2
            for j, part in enumerate((re, im, re + im)):
                high, low = halves(part)
                for q, piece in enumerate((high, low, high)):
                    mid[rows, (3 * j + q) * SIDE : (3 * j + q + 1) * SIDE] = piece
        for m in range(2):
            rows = slice(m * HALF, (m + 1) * HALF)
            p1, p2, p3 = [
                dot(mid[rows, j * K3 : (j + 1) * K3], right[k, j * K3 : (j + 1) * K3, :]) for j in range(3)
            ]
            re = p1 - p2
            im = p3 - p1 - p2
            for q in range(HALF // CH):
                post(m * HALF + q * CH, re[q * CH : (q + 1) * CH], im[q * CH : (q + 1) * CH])

    last = lax.div(d, 3)

    def forward(w):
        @pl.when(d > 0)
        def _():
            fwd_copy(w).wait_recv()

        def mix(i, carry):
            top = pl.multiple_of(i * CH, CH)
            rows = pl.ds(top, CH)
            tr, ti = tmat[0, w, 0, rows, :], tmat[0, w, 1, rows, :]
            xr, xi = hist[0, w, 0, rows, :], hist[0, w, 1, rows, :]
            put(top, tr * xr - ti * xi, tr * xi + ti * xr)
            return carry

        lax.fori_loop(0, STEPS, mix, 0)

        def next_mix(top, xr, xi):
            rows = slice(top, top + CH)
            hist[1, w, 0, rows, :] = xr
            hist[1, w, 1, rows, :] = xi
            tr, ti = tmat[1, w, 0, rows, :], tmat[1, w, 1, rows, :]
            put(top, tr * xr - ti * xi, tr * xi + ti * xr)

        sandwich(0, next_mix)

        def keep(top, xr, xi):
            rows = slice(top, top + CH)
            hist[2, w, 0, rows, :] = xr
            hist[2, w, 1, rows, :] = xi

        sandwich(last, keep)

        @pl.when(d < DEPTH - 1)
        def _():
            fwd_copy(w).start()

        @pl.when(d == DEPTH - 1)
        def _():
            def chunk(i, carry):
                rows = pl.ds(pl.multiple_of(i * CH, CH), CH)
                fr, fi = hist[2, w, 0, rows, :], hist[2, w, 1, rows, :]
                factor = 1.0 - ampv[w, rows, :] / jnp.sqrt(fr * fr + fi * fi + 1.0)
                gin[w, 0, rows, :] = factor * fr
                gin[w, 1, rows, :] = -(factor * fi)
                return carry

            lax.fori_loop(0, STEPS, chunk, 0)

    def backward(w):
        @pl.when(d < DEPTH - 1)
        def _():
            bwd_copy(w).wait_recv()

        def fill(i, carry):
            top = pl.multiple_of(i * CH, CH)
            rows = pl.ds(top, CH)
            put(top, gin[w, 0, rows, :], gin[w, 1, rows, :])
            return carry

        lax.fori_loop(0, STEPS, fill, 0)

        def unmix(s, top, br, bi):
            rows = slice(top, top + CH)
            xr, xi = hist[s, w, 0, rows, :], hist[s, w, 1, rows, :]
            pieces[s, 0, rows, :] = xr * br - xi * bi
            pieces[s, 1, rows, :] = -(xr * bi + xi * br)
            tr, ti = tmat[s, w, 0, rows, :], tmat[s, w, 1, rows, :]
            return tr * br - ti * bi, tr * bi + ti * br

        def upper(top, br, bi):
            put(top, *unmix(1, top, br, bi))

        def lower(top, br, bi):
            re, im = unmix(0, top, br, bi)
            rows = slice(top, top + CH)
            gin[w, 0, rows, :] = re
            gin[w, 1, rows, :] = im

        sandwich(last, upper)
        sandwich(0, lower)

        @pl.when(d > 0)
        def _():
            bwd_copy(w).start()

        @pl.when(d == 0)
        def _():
            r, c = corner(w)
            rows, cols = one_hot(r, True), one_hot(c, False)
            ptot[0] += rolled(gin[w, 0], rows, cols)
            ptot[1] -= rolled(gin[w, 1], rows, cols)

        @pl.when((d == 0) & (w == WINDOWS - 1))
        def _():
            scatter_probe()

        def gather(i, carry):
            rows = pl.ds(pl.multiple_of(i * CH, CH), CH)
            below_r, right_c = masks(i, w)
            for s in range(2):
                for part in range(2):
                    piece = pieces[s, part, rows, :]
                    mine = jnp.where(below_r, piece, 0.0)
                    theirs = jnp.where(below_r, 0.0, piece)
                    acc[s, part, rows, :SIDE] += jnp.where(right_c, mine, 0.0)
                    acc[s, part, rows, SIDE:] += jnp.where(right_c, 0.0, mine)
                    rimacc[s, part, rows, :SIDE] += jnp.where(right_c, theirs, 0.0)
                    rimacc[s, part, rows, SIDE:] += jnp.where(right_c, 0.0, theirs)
            return carry

        lax.fori_loop(0, STEPS, gather, 0)

    tiles = [(q, q // 2, (q % 2) * 128) for q in range(4)]

    def scatter_copy(i):
        return remote(pscat.at[i], pin, ps_s.at[i - 1], ps_r.at[0], {"depth": i})

    def scatter_probe():
        for owner in range(DEPTH):
            for p in range(NZ):
                top = owner * (SIDE // DEPTH) + p * 8
                for q, part, lane in tiles:
                    pscat[owner, p, q] = ptot[part, top : top + 8, lane : lane + 128]
        for owner in range(1, DEPTH):
            scatter_copy(owner).start()
        pin[...] = pscat[0]

    half = lax.div(d, 2)
    lag = (1 - half) * WINDOWS + half * (1 - lax.rem(d, 2))

    def step(k, carry):
        @pl.when(k < WINDOWS)
        def _():
            forward(k)

        b = k - lag

        @pl.when((b >= 0) & (b < WINDOWS))
        def _():
            backward(b)

        return carry

    lax.fori_loop(0, 2 * WINDOWS, step, 0)

    @pl.when(d == 2)
    def _():
        bwd_copy(WINDOWS - 1).wait_send()
        pl.semaphore_signal(go, inc=1, device_id={"tile": above2}, device_id_type=MESH)
        pl.semaphore_wait(go, 1)
        pl.semaphore_signal(go, inc=1, device_id={"depth": 3}, device_id_type=MESH)

    @pl.when(d == 3)
    def _():
        pl.semaphore_wait(go, 1)

    rim_grad_copy(1).start()
    for s in range(2):
        pltpu.make_async_copy(acc.at[s], obj.at[s], obj_sem.at[s]).start()

    @pl.when(d > 0)
    def _():
        scatter_copy(1).wait_recv()

    for i in range(1, NZ):
        to = lax.rem(z + i, NZ)
        remote(pin.at[to], zin.at[i - 1], z_s.at[i - 1], z_r.at[i - 1], {"tile": z_peers[i - 1]}).start()
    total = pin[z]
    for i in range(1, NZ):
        remote(pin.at[0], zin.at[i - 1], z_s.at[i - 1], z_r.at[i - 1], {"tile": z_peers[i - 1]}).wait_recv()
        total = total + zin[i - 1]
    zsum[...] = total
    for i in range(1, NY):
        to = lax.rem(y + i, NY)
        remote(zsum.at[to], yin.at[i - 1], y_s.at[i - 1], y_r.at[i - 1], {"tile": y_peers[i - 1]}).start()
    total = zsum[y]
    for i in range(1, NY):
        remote(zsum.at[0], yin.at[i - 1], y_s.at[i - 1], y_r.at[i - 1], {"tile": y_peers[i - 1]}).wait_recv()
        total = total + yin[i - 1]
    ysum[...] = total
    exchange = remote(ysum, xin, x_s.at[0], x_r.at[0], {"tile": x_peer})
    exchange.start()
    rim_grad_copy(0).start()
    exchange.wait_recv()
    total = total + xin[...]
    xsum[...] = total
    zout[y] = total
    y_back = [
        remote(xsum, zout.at[y], yo_s.at[i - 1], yo_r.at[i - 1], {"tile": y_peers[i - 1]}) for i in range(1, NY)
    ]
    for copy in y_back:
        copy.start()
    for copy in y_back:
        copy.wait_recv()
    pout[z] = zout[...]
    z_back = [
        remote(zout, pout.at[z], zo_s.at[i - 1], zo_r.at[i - 1], {"tile": z_peers[i - 1]}) for i in range(1, NZ)
    ]
    for copy in z_back:
        copy.start()
    for copy in z_back:
        copy.wait_recv()
    for p in range(NZ):
        for q, part, lane in tiles:
            pgrad[part, p * 8 : p * 8 + 8, lane : lane + 128] = pout[p, q]

    for s in (1, 0):
        rim_grad_copy(s).wait_recv()

    @pl.when(d > 0)
    def _():
        rim_copy(0).wait_send()

    rim_copy(1).wait_send()
    for s in range(2):
        rim_grad_copy(s).wait_send()

    @pl.when(d < DEPTH - 1)
    def _():
        for w in range(WINDOWS):
            fwd_copy(w).wait_send()

    @pl.when(d > 0)
    def _():
        for w in range(WINDOWS - 1):
            bwd_copy(w).wait_send()

    @pl.when((d == 1) | (d == 3))
    def _():
        bwd_copy(WINDOWS - 1).wait_send()

    @pl.when(d == 0)
    def _():
        for owner in range(1, DEPTH):
            scatter_copy(owner).wait_send()

    for i in range(1, NZ):
        remote(pin.at[0], zin.at[i - 1], z_s.at[i - 1], z_r.at[i - 1], {"tile": z_peers[i - 1]}).wait_send()
    for i in range(1, NY):
        remote(zsum.at[0], yin.at[i - 1], y_s.at[i - 1], y_r.at[i - 1], {"tile": y_peers[i - 1]}).wait_send()
    exchange.wait_send()
    for copy in y_back + z_back:
        copy.wait_send()
    for s in range(2):
        pltpu.make_async_copy(acc.at[s], obj.at[s], obj_sem.at[s]).wait()


def pinned(x):
    return pltpu.with_memory_space_constraint(x, pltpu.HBM)


def body(transmission, probe_field, scan_positions, amplitudes):
    tables = jnp.asarray(transform_tables())
    vm, dma = pltpu.VMEM, pltpu.SemaphoreType.DMA
    strip = (2, 2, SIDE, 2 * SIDE)
    anywhere = pl.BlockSpec(memory_space=pl.ANY)
    hbm = pl.BlockSpec(memory_space=pltpu.HBM)
    own_terms, rim_terms, probe_grad = pl.pallas_call(
        mega,
        out_shape=(
            jax.ShapeDtypeStruct(transmission.shape, F32),
            jax.ShapeDtypeStruct(transmission.shape, F32),
            jax.ShapeDtypeStruct((2, SIDE // DEPTH, SIDE), F32),
        ),
        in_specs=[hbm, hbm, pl.BlockSpec(memory_space=pltpu.SMEM), hbm, hbm],
        out_specs=(anywhere, anywhere, pl.BlockSpec(memory_space=pltpu.VMEM)),
        scratch_shapes=[
            vm(strip, F32),
            vm(strip, F32),
            vm((2, WINDOWS, 2, SIDE, SIDE), F32),
            vm((3, WINDOWS, 2, SIDE, SIDE), F32),
            vm((WINDOWS, 2, SIDE, SIDE), F32),
            vm((2, 2, SIDE, SIDE), F32),
            vm(strip, F32),
            vm(strip, F32),
            vm((2, SIDE, 9 * SIDE), BF),
            vm((2, 9 * SIDE, SIDE), BF),
            vm((9 * SIDE, SIDE), BF),
            vm((SIDE, 9 * SIDE), BF),
            vm((WINDOWS, SIDE, SIDE), F32),
            vm((2, SIDE, SIDE), F32),
            vm((2, 6, SIDE, SIDE), BF),
            vm((2, SIDE, SIDE), F32),
            vm((DEPTH, NZ, 4, 8, 128), F32),
            vm((NZ, 4, 8, 128), F32),
            vm((NZ - 1, 4, 8, 128), F32),
            vm((4, 8, 128), F32),
            vm((NY - 1, 8, 128), F32),
            vm((8, 128), F32),
            vm((8, 128), F32),
            vm((8, 128), F32),
            vm((4, 8, 128), F32),
            vm((NZ, 4, 8, 128), F32),
            dma((4,)),
            dma((2,)), dma((2,)),
            dma((4,)), dma((4,)),
            dma((4,)), dma((4,)),
            dma((2,)), dma((2,)),
            dma((2,)),
            dma((3,)), dma((1,)),
            dma((7,)), dma((7,)),
            dma((3,)), dma((3,)),
            dma((1,)), dma((1,)),
            dma((3,)), dma((3,)),
            dma((7,)), dma((7,)),
            pltpu.SemaphoreType.REGULAR,
        ],
        compiler_params=pltpu.CompilerParams(
            collective_id=0, has_side_effects=True, vmem_limit_bytes=40 * 1024 * 1024
        ),
    )(pinned(transmission), pinned(probe_field), scan_positions, pinned(amplitudes), pinned(tables))
    return own_terms + rim_terms, probe_grad


def solution(mesh):
    placed = (P("depth", None, "tile", None), P(), P("tile", None), P("tile", None, None))
    return jax.shard_map(
        body,
        mesh=mesh,
        in_specs=placed,
        out_specs=(P("depth", None, "tile", None), P(None, "depth", None)),
        check_vma=False,
    )
```

```python
import jax
import jax.numpy as jnp
import ml_dtypes
import numpy as np
from jax import lax
from jax.experimental import pallas as pl
from jax.experimental.pallas import tpu as pltpu
from jax.sharding import PartitionSpec as P

MESH = pl.DeviceIdType.MESH
BF = jnp.bfloat16
F32 = jnp.float32
SIDE = 256
DEPTH = 4
WINDOWS = 4
NY, NZ, NX = 4, 8, 2
TILES = NY * NZ * NX
CH = 32
STEPS = SIDE // CH


def transform_tables():
    n = np.arange(SIDE)
    dft = np.exp(-2j * np.pi * ((n[:, None] * n[None, :]) % SIDE) / SIDE)
    m = np.where(n < SIDE // 2, n, n - SIDE).astype(np.float64)
    phase = np.exp(-1j * np.pi * m * m / (4 * SIDE))
    fresnel = (np.conj(dft) * phase[None, :]) @ dft / SIDE
    far = dft / np.sqrt(SIDE)
    pieces = []
    for table in (fresnel, far):
        for part in (table.real, table.imag, table.real + table.imag):
            high = part.astype(np.float32).astype(ml_dtypes.bfloat16)
            low = (part - high.astype(np.float64)).astype(np.float32)
            pieces += [high, low.astype(ml_dtypes.bfloat16)]
    return np.stack(pieces).reshape(2, 6, SIDE, SIDE)


def halves(x):
    high = x.astype(BF)
    return high, (x - high.astype(F32)).astype(BF)


def thirds(x):
    high = x.astype(BF)
    rest = x - high.astype(F32)
    mid = rest.astype(BF)
    return high, mid, (rest - mid.astype(F32)).astype(BF)


def mega(
    trans, probe, pos, amp, tabs, obj, rimg, pgrad,
    own, rim, tmat, hist, gin, pieces, acc, rimacc, left, right, dat, mid,
    ampv, probev, tabv, ptot, pscat, pin, zin, zsum, yin, ysum, xin, xsum, zout, pout,
    local_sem, rim_s, rim_r, fwd_s, fwd_r, bwd_s, bwd_r, rg_s, rg_r, obj_sem,
    ps_s, ps_r, z_s, z_r, y_s, y_r, x_s, x_r, yo_s, yo_r, zo_s, zo_r, go,
):
    d = lax.axis_index("depth")
    t = lax.axis_index("tile")
    xh = lax.rem(t, NX)
    z = lax.rem(lax.div(t, NX), NZ)
    y = lax.div(t, NX * NZ)
    above = lax.rem(t + TILES - 1, TILES)
    below = lax.rem(t + 1, TILES)

    def tile_of(yy, zz, xx):
        return (yy * NZ + zz) * NX + xx

    z_peers = [tile_of(y, lax.rem(z + i, NZ), xh) for i in range(1, NZ)]
    y_peers = [tile_of(lax.rem(y + i, NY), z, xh) for i in range(1, NY)]
    x_peer = tile_of(y, z, 1 - xh)

    barrier = pltpu.get_barrier_semaphore()
    above2 = lax.rem(t + TILES - 2, TILES)
    below2 = lax.rem(t + 2, TILES)
    peers = [{"tile": p} for p in [above, below, above2, below2] + z_peers + y_peers]
    peers += [{"depth": lax.rem(d + i, DEPTH)} for i in range(1, DEPTH)]
    for peer in peers:
        pl.semaphore_signal(barrier, inc=1, device_id=peer, device_id_type=MESH)
    pl.semaphore_wait(barrier, len(peers))

    def remote(src, dst, ss, rs, peer):
        return pltpu.make_async_remote_copy(src, dst, ss, rs, device_id=peer, device_id_type=MESH)

    def rim_copy(s):
        return remote(trans.at[s], rim.at[s], rim_s.at[s], rim_r.at[s], {"tile": above})

    def rim_grad_copy(s):
        return remote(rimacc.at[s], rimg.at[s], rg_s.at[s], rg_r.at[s], {"tile": below})

    def fwd_copy(w):
        return remote(hist.at[2, w], hist.at[0, w], fwd_s.at[w], fwd_r.at[w], {"depth": lax.rem(d + 1, DEPTH)})

    def bwd_copy(w):
        return remote(gin.at[w], gin.at[w], bwd_s.at[w], bwd_r.at[w], {"depth": lax.rem(d + DEPTH - 1, DEPTH)})

    @pl.when(d != 1)
    def _():
        for s in range(2):
            rim_copy(s).start()

    loads = [
        pltpu.make_async_copy(tabs, tabv, local_sem.at[0]),
        pltpu.make_async_copy(probe, probev, local_sem.at[1]),
        pltpu.make_async_copy(trans, own, local_sem.at[2]),
        pltpu.make_async_copy(amp, ampv, local_sem.at[3]),
    ]
    for load in loads:
        load.start()

    def clear(i, carry):
        rows = pl.ds(pl.multiple_of(i * CH, CH), CH)
        for s in range(2):
            for part in range(2):
                acc[s, part, rows, :] = jnp.zeros((CH, 2 * SIDE), F32)
                rimacc[s, part, rows, :] = jnp.zeros((CH, 2 * SIDE), F32)
        for part in range(2):
            ptot[part, rows, :] = jnp.zeros((CH, SIDE), F32)
        return carry

    lax.fori_loop(0, STEPS, clear, 0)
    loads[0].wait()
    for k in range(2):
        for j in range(3):
            high, low = tabv[k, 2 * j], tabv[k, 2 * j + 1]
            for q, piece in enumerate((high, high, low)):
                span = slice((3 * j + q) * SIDE, (3 * j + q + 1) * SIDE)
                left[k, :, span] = piece
                right[k, span, :] = piece

    @pl.when(d == 0)
    def _():
        rim_copy(0).wait_send()
        pl.semaphore_signal(go, inc=1, device_id={"depth": 1}, device_id_type=MESH)

    @pl.when(d == 1)
    def _():
        pl.semaphore_wait(go, 1)
        for s in range(2):
            rim_copy(s).start()

    loads[1].wait()
    loads[2].wait()
    loads[3].wait()

    def corner(w):
        return pos[0, w] - t * SIDE, pos[1, w]

    def one_hot(shift, flip):
        row = lax.broadcasted_iota(jnp.int32, (SIDE, SIDE), 0)
        col = lax.broadcasted_iota(jnp.int32, (SIDE, SIDE), 1)
        gap = (col - row) if flip else (row - col)
        return jnp.where(((gap - shift) & (SIDE - 1)) == 0, 1.0, 0.0).astype(BF)

    def rolled(x, rows, cols):
        a = sum(jnp.dot(rows, piece, preferred_element_type=F32) for piece in thirds(x))
        return sum(jnp.dot(piece, cols, preferred_element_type=F32) for piece in thirds(a))

    @pl.when(d == 0)
    def _():
        def place(w, carry):
            r, c = corner(w)
            rows, cols = one_hot(r, False), one_hot(c, True)
            for part in range(2):
                hist[0, w, part] = rolled(probev[part], rows, cols)
            return carry

        lax.fori_loop(0, WINDOWS, place, 0)

    def masks(i, w):
        r, c = corner(w)
        row = lax.broadcasted_iota(jnp.int32, (CH, SIDE), 0) + i * CH
        col = lax.broadcasted_iota(jnp.int32, (CH, SIDE), 1)
        return row >= r, col >= c

    for s in range(2):
        rim_copy(s).wait_recv()

        def crop(w, carry, s=s):
            def chunk(i, carry2):
                rows = pl.ds(pl.multiple_of(i * CH, CH), CH)
                below_r, right_c = masks(i, w)
                for part in range(2):
                    mine = jnp.where(right_c, own[s, part, rows, :SIDE], own[s, part, rows, SIDE:])
                    theirs = jnp.where(right_c, rim[s, part, rows, :SIDE], rim[s, part, rows, SIDE:])
                    tmat[s, w, part, rows, :] = jnp.where(below_r, mine, theirs)
                return carry2

            return lax.fori_loop(0, STEPS, chunk, carry)

        lax.fori_loop(0, WINDOWS, crop, 0)

    def put(top, re, im):
        size = re.shape[0]
        for j, part in enumerate((re, im, re + im)):
            high, low = halves(part)
            for q, piece in enumerate((high, low, high)):
                start = (3 * j + q) * SIDE + top
                if not isinstance(top, int):
                    start = pl.multiple_of(start, CH)
                dat[pl.ds(start, size), :] = piece

    def dot(a, b):
        return jnp.dot(a, b, preferred_element_type=F32)

    K3 = 3 * SIDE
    HALF = SIDE // 2

    def sandwich(k, post):
        for m in range(2):
            rows = slice(m * HALF, (m + 1) * HALF)
            p1, p2, p3 = [
                dot(left[k, rows, j * K3 : (j + 1) * K3], dat[j * K3 : (j + 1) * K3, :]) for j in range(3)
            ]
            re = p1 - p2
            im = p3 - p1 - p2
            for j, part in enumerate((re, im, re + im)):
                high, low = halves(part)
                for q, piece in enumerate((high, low, high)):
                    mid[rows, (3 * j + q) * SIDE : (3 * j + q + 1) * SIDE] = piece
        for m in range(2):
            rows = slice(m * HALF, (m + 1) * HALF)
            p1, p2, p3 = [
                dot(mid[rows, j * K3 : (j + 1) * K3], right[k, j * K3 : (j + 1) * K3, :]) for j in range(3)
            ]
            re = p1 - p2
            im = p3 - p1 - p2
            for q in range(HALF // CH):
                post(m * HALF + q * CH, re[q * CH : (q + 1) * CH], im[q * CH : (q + 1) * CH])

    last = lax.div(d, 3)

    def forward(w):
        @pl.when(d > 0)
        def _():
            fwd_copy(w).wait_recv()

        def mix(i, carry):
            top = pl.multiple_of(i * CH, CH)
            rows = pl.ds(top, CH)
            tr, ti = tmat[0, w, 0, rows, :], tmat[0, w, 1, rows, :]
            xr, xi = hist[0, w, 0, rows, :], hist[0, w, 1, rows, :]
            put(top, tr * xr - ti * xi, tr * xi + ti * xr)
            return carry

        lax.fori_loop(0, STEPS, mix, 0)

        def next_mix(top, xr, xi):
            rows = slice(top, top + CH)
            hist[1, w, 0, rows, :] = xr
            hist[1, w, 1, rows, :] = xi
            tr, ti = tmat[1, w, 0, rows, :], tmat[1, w, 1, rows, :]
            put(top, tr * xr - ti * xi, tr * xi + ti * xr)

        sandwich(0, next_mix)

        def keep(top, xr, xi):
            rows = slice(top, top + CH)
            hist[2, w, 0, rows, :] = xr
            hist[2, w, 1, rows, :] = xi

        sandwich(last, keep)

        @pl.when(d < DEPTH - 1)
        def _():
            fwd_copy(w).start()

        @pl.when(d == DEPTH - 1)
        def _():
            def chunk(i, carry):
                rows = pl.ds(pl.multiple_of(i * CH, CH), CH)
                fr, fi = hist[2, w, 0, rows, :], hist[2, w, 1, rows, :]
                factor = 1.0 - ampv[w, rows, :] / jnp.sqrt(fr * fr + fi * fi + 1.0)
                gin[w, 0, rows, :] = factor * fr
                gin[w, 1, rows, :] = -(factor * fi)
                return carry

            lax.fori_loop(0, STEPS, chunk, 0)

    def backward(w):
        @pl.when(d < DEPTH - 1)
        def _():
            bwd_copy(w).wait_recv()

        def fill(i, carry):
            top = pl.multiple_of(i * CH, CH)
            rows = pl.ds(top, CH)
            put(top, gin[w, 0, rows, :], gin[w, 1, rows, :])
            return carry

        lax.fori_loop(0, STEPS, fill, 0)

        def unmix(s, top, br, bi):
            rows = slice(top, top + CH)
            xr, xi = hist[s, w, 0, rows, :], hist[s, w, 1, rows, :]
            pieces[s, 0, rows, :] = xr * br - xi * bi
            pieces[s, 1, rows, :] = -(xr * bi + xi * br)
            tr, ti = tmat[s, w, 0, rows, :], tmat[s, w, 1, rows, :]
            return tr * br - ti * bi, tr * bi + ti * br

        def upper(top, br, bi):
            put(top, *unmix(1, top, br, bi))

        def lower(top, br, bi):
            re, im = unmix(0, top, br, bi)
            rows = slice(top, top + CH)
            gin[w, 0, rows, :] = re
            gin[w, 1, rows, :] = im

        sandwich(last, upper)
        sandwich(0, lower)

        @pl.when(d > 0)
        def _():
            bwd_copy(w).start()

        @pl.when(d == 0)
        def _():
            r, c = corner(w)
            rows, cols = one_hot(r, True), one_hot(c, False)
            ptot[0] += rolled(gin[w, 0], rows, cols)
            ptot[1] -= rolled(gin[w, 1], rows, cols)

        @pl.when((d == 0) & (w == WINDOWS - 1))
        def _():
            scatter_probe()

        def gather(i, carry):
            rows = pl.ds(pl.multiple_of(i * CH, CH), CH)
            below_r, right_c = masks(i, w)
            for s in range(2):
                for part in range(2):
                    piece = pieces[s, part, rows, :]
                    mine = jnp.where(below_r, piece, 0.0)
                    theirs = jnp.where(below_r, 0.0, piece)
                    acc[s, part, rows, :SIDE] += jnp.where(right_c, mine, 0.0)
                    acc[s, part, rows, SIDE:] += jnp.where(right_c, 0.0, mine)
                    rimacc[s, part, rows, :SIDE] += jnp.where(right_c, theirs, 0.0)
                    rimacc[s, part, rows, SIDE:] += jnp.where(right_c, 0.0, theirs)
            return carry

        lax.fori_loop(0, STEPS, gather, 0)

    tiles = [(q, q // 2, (q % 2) * 128) for q in range(4)]

    def scatter_copy(i):
        return remote(pscat.at[i], pin, ps_s.at[i - 1], ps_r.at[0], {"depth": i})

    def scatter_probe():
        for owner in range(DEPTH):
            for p in range(NZ):
                top = owner * (SIDE // DEPTH) + p * 8
                for q, part, lane in tiles:
                    pscat[owner, p, q] = ptot[part, top : top + 8, lane : lane + 128]
        for owner in range(1, DEPTH):
            scatter_copy(owner).start()
        pin[...] = pscat[0]

    half = lax.div(d, 2)
    lag = (1 - half) * WINDOWS + half * (1 - lax.rem(d, 2))

    def step(k, carry):
        @pl.when(k < WINDOWS)
        def _():
            forward(k)

        b = k - lag

        @pl.when((b >= 0) & (b < WINDOWS))
        def _():
            backward(b)

        return carry

    lax.fori_loop(0, 2 * WINDOWS, step, 0)

    @pl.when(d == 2)
    def _():
        bwd_copy(WINDOWS - 1).wait_send()
        pl.semaphore_signal(go, inc=1, device_id={"tile": above2}, device_id_type=MESH)
        pl.semaphore_wait(go, 1)
        pl.semaphore_signal(go, inc=1, device_id={"depth": 3}, device_id_type=MESH)

    @pl.when(d == 3)
    def _():
        pl.semaphore_wait(go, 1)

    rim_grad_copy(1).start()

    @pl.when(d == 3)
    def _():
        rim_grad_copy(0).start()

    for s in range(2):
        pltpu.make_async_copy(acc.at[s], obj.at[s], obj_sem.at[s]).start()

    @pl.when(d > 0)
    def _():
        scatter_copy(1).wait_recv()

    for i in range(1, NZ):
        to = lax.rem(z + i, NZ)
        remote(pin.at[to], zin.at[i - 1], z_s.at[i - 1], z_r.at[i - 1], {"tile": z_peers[i - 1]}).start()
    total = pin[z]
    for i in range(1, NZ):
        remote(pin.at[0], zin.at[i - 1], z_s.at[i - 1], z_r.at[i - 1], {"tile": z_peers[i - 1]}).wait_recv()
        total = total + zin[i - 1]
    zsum[...] = total
    for i in range(1, NY):
        to = lax.rem(y + i, NY)
        remote(zsum.at[to], yin.at[i - 1], y_s.at[i - 1], y_r.at[i - 1], {"tile": y_peers[i - 1]}).start()
    total = zsum[y]
    for i in range(1, NY):
        remote(zsum.at[0], yin.at[i - 1], y_s.at[i - 1], y_r.at[i - 1], {"tile": y_peers[i - 1]}).wait_recv()
        total = total + yin[i - 1]
    ysum[...] = total
    exchange = remote(ysum, xin, x_s.at[0], x_r.at[0], {"tile": x_peer})
    exchange.start()

    @pl.when(d < 3)
    def _():
        rim_grad_copy(0).start()

    exchange.wait_recv()
    total = total + xin[...]
    xsum[...] = total
    zout[y] = total
    y_back = [
        remote(xsum, zout.at[y], yo_s.at[i - 1], yo_r.at[i - 1], {"tile": y_peers[i - 1]}) for i in range(1, NY)
    ]
    for copy in y_back:
        copy.start()
    for copy in y_back:
        copy.wait_recv()
    pout[z] = zout[...]
    z_back = [
        remote(zout, pout.at[z], zo_s.at[i - 1], zo_r.at[i - 1], {"tile": z_peers[i - 1]}) for i in range(1, NZ)
    ]
    for copy in z_back:
        copy.start()
    for copy in z_back:
        copy.wait_recv()
    for p in range(NZ):
        for q, part, lane in tiles:
            pgrad[part, p * 8 : p * 8 + 8, lane : lane + 128] = pout[p, q]

    for s in (1, 0):
        rim_grad_copy(s).wait_recv()

    @pl.when(d > 0)
    def _():
        rim_copy(0).wait_send()

    rim_copy(1).wait_send()
    for s in range(2):
        rim_grad_copy(s).wait_send()

    @pl.when(d < DEPTH - 1)
    def _():
        for w in range(WINDOWS):
            fwd_copy(w).wait_send()

    @pl.when(d > 0)
    def _():
        for w in range(WINDOWS - 1):
            bwd_copy(w).wait_send()

    @pl.when((d == 1) | (d == 3))
    def _():
        bwd_copy(WINDOWS - 1).wait_send()

    @pl.when(d == 0)
    def _():
        for owner in range(1, DEPTH):
            scatter_copy(owner).wait_send()

    for i in range(1, NZ):
        remote(pin.at[0], zin.at[i - 1], z_s.at[i - 1], z_r.at[i - 1], {"tile": z_peers[i - 1]}).wait_send()
    for i in range(1, NY):
        remote(zsum.at[0], yin.at[i - 1], y_s.at[i - 1], y_r.at[i - 1], {"tile": y_peers[i - 1]}).wait_send()
    exchange.wait_send()
    for copy in y_back + z_back:
        copy.wait_send()
    for s in range(2):
        pltpu.make_async_copy(acc.at[s], obj.at[s], obj_sem.at[s]).wait()


def pinned(x):
    return pltpu.with_memory_space_constraint(x, pltpu.HBM)


def body(transmission, probe_field, scan_positions, amplitudes):
    tables = jnp.asarray(transform_tables())
    vm, dma = pltpu.VMEM, pltpu.SemaphoreType.DMA
    strip = (2, 2, SIDE, 2 * SIDE)
    anywhere = pl.BlockSpec(memory_space=pl.ANY)
    hbm = pl.BlockSpec(memory_space=pltpu.HBM)
    own_terms, rim_terms, probe_grad = pl.pallas_call(
        mega,
        out_shape=(
            jax.ShapeDtypeStruct(transmission.shape, F32),
            jax.ShapeDtypeStruct(transmission.shape, F32),
            jax.ShapeDtypeStruct((2, SIDE // DEPTH, SIDE), F32),
        ),
        in_specs=[hbm, hbm, pl.BlockSpec(memory_space=pltpu.SMEM), hbm, hbm],
        out_specs=(anywhere, anywhere, pl.BlockSpec(memory_space=pltpu.VMEM)),
        scratch_shapes=[
            vm(strip, F32),
            vm(strip, F32),
            vm((2, WINDOWS, 2, SIDE, SIDE), F32),
            vm((3, WINDOWS, 2, SIDE, SIDE), F32),
            vm((WINDOWS, 2, SIDE, SIDE), F32),
            vm((2, 2, SIDE, SIDE), F32),
            vm(strip, F32),
            vm(strip, F32),
            vm((2, SIDE, 9 * SIDE), BF),
            vm((2, 9 * SIDE, SIDE), BF),
            vm((9 * SIDE, SIDE), BF),
            vm((SIDE, 9 * SIDE), BF),
            vm((WINDOWS, SIDE, SIDE), F32),
            vm((2, SIDE, SIDE), F32),
            vm((2, 6, SIDE, SIDE), BF),
            vm((2, SIDE, SIDE), F32),
            vm((DEPTH, NZ, 4, 8, 128), F32),
            vm((NZ, 4, 8, 128), F32),
            vm((NZ - 1, 4, 8, 128), F32),
            vm((4, 8, 128), F32),
            vm((NY - 1, 8, 128), F32),
            vm((8, 128), F32),
            vm((8, 128), F32),
            vm((8, 128), F32),
            vm((4, 8, 128), F32),
            vm((NZ, 4, 8, 128), F32),
            dma((4,)),
            dma((2,)), dma((2,)),
            dma((4,)), dma((4,)),
            dma((4,)), dma((4,)),
            dma((2,)), dma((2,)),
            dma((2,)),
            dma((3,)), dma((1,)),
            dma((7,)), dma((7,)),
            dma((3,)), dma((3,)),
            dma((1,)), dma((1,)),
            dma((3,)), dma((3,)),
            dma((7,)), dma((7,)),
            pltpu.SemaphoreType.REGULAR,
        ],
        compiler_params=pltpu.CompilerParams(
            collective_id=0, has_side_effects=True, vmem_limit_bytes=40 * 1024 * 1024
        ),
    )(pinned(transmission), pinned(probe_field), scan_positions.T, pinned(amplitudes), pinned(tables))
    return own_terms + rim_terms, probe_grad


def solution(mesh):
    placed = (P("depth", None, "tile", None), P(), P("tile", None), P("tile", None, None))
    return jax.shard_map(
        body,
        mesh=mesh,
        in_specs=placed,
        out_specs=(P("depth", None, "tile", None), P(None, "depth", None)),
        check_vma=False,
    )
```
